32 devices in a mesh: rep: 4 (over y, core), shard: 8 (over z, x).
Axes of the slice: x: 2, y: 2, z: 4, core: 2. Of those that a mesh axis runs over, the one named last changes fastest.
Arguments:
- weights: bfloat16 [4, 4096, 5120], P('rep', 'shard'), may hold values from -12 to 12
- warm_start: bfloat16 [4, 2, 16, 5120], P('rep'), may hold values from -4 to 4, as said below
Outputs:
- corrected: bfloat16 [4, 4096, 5120], P('rep', 'shard')
- factors: float32 [4, 2, 16, 5120], P('rep')
The draws below stay inside these ranges and needn't reach their ends.
Inputs may be any that keep to these rules, and one draw needn't show every extreme that they name: `warm_start`: replicas whose indices differ only in bit 0 hold equal start vectors for matching 0, and replicas whose indices differ by 2 hold equal start vectors for matching 1.
All inputs are finite; a program needn't handle non-finite values.
Results may differ from the reference program's by a relative error of at most 0.0049.
Values sent between devices are 32-bit elements; how exact they have to be, the bound alone decides.
A program may use at most 64 MiB of HBM per device.

```python
import jax
import jax.numpy as jnp
import numpy as np
from jax import lax

ROWS = 4096
COLS = 5120
RANK = 16
STEPS = 2
REP = 4
HALF_REP = 2


def draw_weights(key, part):
    noise_key, scale_key = jax.random.split(jax.random.fold_in(key, 11))
    values = jnp.clip(jax.random.normal(noise_key, (REP, ROWS, COLS), jnp.float32), -4.0, 4.0)
    position = jnp.arange(ROWS).astype(jnp.float32) / ROWS
    roughness = jnp.exp(jax.random.uniform(scale_key, (REP, ROWS, 1), jnp.float32, 0.0, 1.2))
    row_scale = 0.3 * jnp.exp(jnp.log(3.0) * position)[None, :, None] * roughness
    return (values * row_scale).astype(jnp.bfloat16)


def draw_warm_start(key, part):
    noise_key = jax.random.fold_in(key, 23)
    values = jnp.clip(jax.random.normal(noise_key, (REP, STEPS, RANK, COLS), jnp.float32), -4.0, 4.0)
    replica = jnp.arange(REP)
    first_pair = replica - replica % 2
    second_pair = replica % HALF_REP
    return jnp.stack([values[first_pair, 0], values[second_pair, 1]], axis=1).astype(jnp.bfloat16)


def setup_inputs(seed: int = 0) -> dict:
    seeds = jax.random.split(jax.random.key(seed), 3)
    return {
        "weights": draw_weights(jax.random.fold_in(seeds[2], 71), 0),
        "warm_start": draw_warm_start(jax.random.fold_in(seeds[2], 71), 0),
    }


def partner_table(matching):
    replica = np.arange(REP)
    if matching == 0:
        return (replica ^ 1, 1.0 - 2.0 * (replica % 2))
    return (replica ^ HALF_REP, 1.0 - 2.0 * (replica // HALF_REP))

def project_rows(operands):
    return lax.dot_general(operands[0].astype(jnp.float32), operands[1].astype(jnp.float32), (((1,), (1,)), ((), ())), preferred_element_type=jnp.float32)

def project_back(operands):
    return jnp.dot(operands[0].astype(jnp.float32), operands[1].astype(jnp.float32), preferred_element_type=jnp.float32)

def apply_update(operands):
    weight_block, basis_rows, factor_rows, sign_value = operands
    change = lax.dot_general(basis_rows, factor_rows, (((0,), (0,)), ((), ())), precision=lax.Precision.HIGHEST)
    return (weight_block.astype(jnp.float32) - 0.5 * sign_value * change).astype(jnp.bfloat16)

def reference(weights, warm_start):
    current = weights
    factor_list = []
    for matching in range(STEPS):
        partner, parity = partner_table(matching)
        sign_values = jnp.asarray(parity, jnp.float32)
        sign_column = sign_values[:, None, None]
        starts = warm_start[:, matching]
        sketch = lax.map(project_rows, (starts, current))
        differ = sign_column * (sketch - sketch[partner])
        gram_sum = jnp.einsum('rkn,rln->rkl', differ, differ, precision=lax.Precision.HIGHEST)
        triangle = jnp.linalg.cholesky(gram_sum)
        basis_rows = lax.linalg.triangular_solve(triangle, differ, left_side=True, lower=True)
        basis_half = basis_rows.astype(jnp.bfloat16)
        signed = sign_column * lax.map(project_back, (basis_half, current))
        factors = signed + signed[partner]
        current = lax.map(apply_update, (current, basis_rows, factors, sign_values))
        factor_list.append(factors)
    return (current, jnp.stack(factor_list, axis=1))
```

```python
import functools
import math

import jax
import jax.numpy as jnp
from jax import lax
from jax.experimental import pallas as pl
from jax.experimental.pallas import tpu as pltpu
from jax.sharding import PartitionSpec as P

STEPS = 2
LANES = 128
F32 = jnp.float32
BF16 = jnp.bfloat16
NT = (((1,), (1,)), ((), ()))


def split(value):
    high = value.astype(BF16).astype(F32)
    return high, value - high


def stack_left(basis, scale):
    high, low = split(scale * basis)
    rank, rows = basis.shape
    pad = jnp.zeros((LANES - 3 * rank, rows), F32)
    return jnp.concatenate([high, high, low, pad], axis=0).T.astype(BF16)


def stack_right(factor):
    high, low = split(factor)
    rank, cols = factor.shape
    pad = jnp.zeros((LANES - 3 * rank, cols), F32)
    return jnp.concatenate([high, low, high, pad], axis=0).astype(BF16)


def whiten(gram, differ):
    rank = differ.shape[0]
    row = lax.broadcasted_iota(jnp.int32, (rank, 1), 0)
    pivots = jnp.ones((rank, 1), F32)
    for k in range(rank):
        pivot = gram[k : k + 1, k : k + 1]
        pivots = jnp.where(row == k, pivot, pivots)
        if k == rank - 1:
            break
        column = jnp.where(row > k, gram[:, k : k + 1] / pivot, 0.0)
        gram = gram - column * gram[k : k + 1, :]
        differ = differ - column * differ[k : k + 1, :]
    return differ / jnp.sqrt(pivots)


def comm_kernel(
    nrep, nsh, nown,
    w_hbm, starts, cur_out, fac_out, bt_out,
    cur, sk, skin, gbuf, pbuf, pin, psum, rsbuf, fac, bt,
    ld_sem, st_sem, fo_sem, sk_s, sk_r, g_s, g_r, p_s, p_r, rs_s, rs_r, ag_s, ag_r, fw_s, fw_r,
):
    rows, cols = cur.shape
    rank = starts.shape[1]
    half_rank = rank // 2
    width = cols // nown
    stride = nsh // nown
    half = nrep // 2
    me_r = lax.axis_index("rep")
    me_s = lax.axis_index("shard")
    me_j = me_s // stride
    bits = (me_r % 2, me_r // half)
    partners = (me_r + 1 - 2 * (me_r % 2), (me_r + half) % nrep)
    signs = tuple((1 - 2 * b).astype(F32) for b in bits)

    def where(j):
        return pl.ds(pl.multiple_of(j * width, LANES), width)

    def load(c):
        return pltpu.make_async_copy(
            w_hbm.at[:, pl.ds(c * width, width)], cur.at[:, pl.ds(c * width, width)], ld_sem.at[c]
        )

    def remote(src, dst, ssem, rsem, rep, shard):
        return pltpu.make_async_remote_copy(
            src_ref=src, dst_ref=dst, send_sem=ssem, recv_sem=rsem,
            device_id={"rep": rep, "shard": shard}, device_id_type=pl.DeviceIdType.MESH,
        )

    def owner(fn, negate=False):
        if stride == 1:
            if not negate:
                fn()
        else:
            here = me_s % stride != 0 if negate else me_s % stride == 0
            pl.when(here)(fn)

    for c in range(nown):
        load(c).start()

    barrier = pltpu.get_barrier_semaphore()
    for o in range(1, nsh):
        pl.semaphore_signal(
            barrier, inc=1, device_id={"rep": me_r, "shard": (me_s + o) % nsh},
            device_id_type=pl.DeviceIdType.MESH,
        )
    for p in partners:
        pl.semaphore_signal(
            barrier, inc=1, device_id={"rep": p, "shard": me_s},
            device_id_type=pl.DeviceIdType.MESH,
        )

    sketch = jnp.zeros((rank, rows), F32)
    for c in range(nown):
        load(c).wait()
        part = pl.ds(c * width, width)
        sketch = sketch + lax.dot_general(
            starts[0, :, part], cur[:, part], NT, preferred_element_type=F32
        )
    pl.semaphore_wait(barrier, nsh - 1 + 2)

    for k in range(STEPS):
        bit, mate, sign = bits[k], partners[k], signs[k]
        sk[k] = sketch
        swap = remote(sk.at[k], skin.at[k], sk_s.at[k], sk_r.at[k], mate, me_s)
        swap.start()
        swap.wait_recv()
        differ = sign * (sketch - skin[k])
        wide = jnp.concatenate([differ, jnp.zeros((LANES - rank, rows), F32)], axis=0)
        gram = lax.dot_general(
            differ, wide, NT, precision=lax.Precision.HIGHEST, preferred_element_type=F32
        )
        gbuf[k, me_s] = gram[:half_rank] + pltpu.roll(gram[half_rank:], rank, 1)

        def gsend(o):
            other = (me_s + o) % nsh
            return remote(
                gbuf.at[k, me_s], gbuf.at[k, me_s], g_s.at[k, other], g_r.at[k, me_s], me_r, other
            )

        def gwait(o):
            other = (me_s + o) % nsh
            return remote(
                gbuf.at[k, other], gbuf.at[k, other], g_s.at[k, other], g_r.at[k, other], me_r, other
            )

        for o in range(1, nsh):
            gsend(o).start()
        for o in range(1, nsh):
            gwait(o).wait_recv()
        total = gbuf[k, 0]
        for s in range(1, nsh):
            total = total + gbuf[k, s]
        gram = jnp.concatenate([total, pltpu.roll(total, LANES - rank, 1)], axis=0)
        basis = whiten(gram, differ)
        basis_half = basis.astype(BF16)

        def psend(j):
            return remote(
                pbuf.at[k, 1 - bit, :, where(j)], pin.at[k, j], p_s.at[k, j], p_r.at[k, j], mate, me_s
            )

        def rsend(j):
            return remote(
                psum.at[k, j], rsbuf.at[k, me_s], rs_s.at[k, j], rs_r.at[k, me_s], me_r, j * stride
            )

        def rwait(o):
            other = (me_s + o) % nsh
            return remote(
                rsbuf.at[k, other], rsbuf.at[k, other], rs_s.at[k, 0], rs_r.at[k, other], me_r, other
            )

        def asend(o):
            other = (me_s + o) % nsh
            piece = fac.at[k, bit, :, where(me_j)]
            return remote(piece, piece, ag_s.at[k, other], ag_r.at[k, me_j], me_r, other)

        def await_piece(j):
            piece = fac.at[k, bit, :, where(j)]
            return remote(piece, piece, ag_s.at[k, 0], ag_r.at[k, j], me_r, j * stride)

        def fsend(j):
            piece = fac.at[k, bit, :, where(j)]
            return remote(piece, piece, fw_s.at[k, j], fw_r.at[k, j], mate, me_s)

        def fwait(j):
            piece = fac.at[k, 1 - bit, :, where(j)]
            return remote(piece, piece, fw_s.at[k, j], fw_r.at[k, j], mate, me_s)

        order = [(me_j + 1 + i) % nown for i in range(nown)]

        def pass_on(i):
            j = order[i]
            psend(j).wait_recv()
            psum[k, j] = pbuf[k, bit, :, where(j)] + pin[k, j]
            if i < nown - 1:
                rsend(j).start()
            else:
                owner(lambda: rsend(j).start(), negate=True)

        lag = 2
        for i in range(nown):
            j = order[i]
            product = sign * jnp.dot(
                basis_half, cur[:, where(j)], preferred_element_type=F32
            )
            pbuf[k, 0, :, where(j)] = product[:half_rank]
            pbuf[k, 1, :, where(j)] = product[half_rank:]
            psend(j).start()
            if i >= lag:
                pass_on(i - lag)
        for i in range(max(nown - lag, 0), nown):
            pass_on(i)
        bt[k] = stack_left(basis, -0.5 * sign)

        def reduce_and_send():
            for o in range(1, nsh):
                rwait(o).wait_recv()
            total = psum[k, me_j]
            for o in range(1, nsh):
                total = total + rsbuf[k, (me_s + o) % nsh]
            fac[k, bit, :, where(me_j)] = total
            for o in range(1, nsh):
                asend(o).start()

        owner(reduce_and_send)
        owner(lambda: await_piece(me_j).wait_recv(), negate=True)
        fsend(me_j).start()
        if k + 1 < STEPS:
            sketch = jnp.zeros((rank, rows), F32)

        def take(i, sketch):
            j = (me_j + i) % nown
            fwait(j).wait_recv()
            if k + 1 == STEPS:
                return sketch
            piece = jnp.concatenate([fac[k, 0, :, where(j)], fac[k, 1, :, where(j)]], axis=0)
            change = jnp.dot(bt[k], stack_right(piece), preferred_element_type=F32)
            fresh = (cur[:, where(j)].astype(F32) + change).astype(BF16)
            cur[:, where(j)] = fresh
            pltpu.make_async_copy(
                cur.at[:, where(j)], cur_out.at[:, where(j)], st_sem.at[j]
            ).start()
            return sketch + lax.dot_general(
                starts[k + 1, :, where(j)], fresh, NT, preferred_element_type=F32
            )

        for i in range(1, nown):
            j = (me_j + i) % nown
            await_piece(j).wait_recv()
            fsend(j).start()
            if i >= lag:
                sketch = take(i - lag, sketch)
        for i in range(max(nown - lag, 0), nown):
            sketch = take(i, sketch)

        pltpu.make_async_copy(fac.at[k], fac_out.at[k], fo_sem.at[k]).start()
        swap.wait_send()
        for o in range(1, nsh):
            gsend(o).wait_send()
        for i in range(nown):
            psend(order[i]).wait_send()
            fsend(order[i]).wait_send()
            if i < nown - 1:
                rsend(order[i]).wait_send()
        owner(lambda: rsend(me_j).wait_send(), negate=True)

        def sent_all():
            for o in range(1, nsh):
                asend(o).wait_send()

        owner(sent_all)

    bt_out[...] = bt[STEPS - 1]
    for k in range(STEPS):
        pltpu.make_async_copy(fac.at[k], fac_out.at[k], fo_sem.at[k]).wait()
    for j in range(nown):
        pltpu.make_async_copy(cur.at[:, where(j)], cur_out.at[:, where(j)], st_sem.at[j]).wait()


def update_kernel(cur, bt, fac, out):
    change = jnp.dot(bt[...], stack_right(fac[...]), preferred_element_type=F32)
    out[...] = (cur[...].astype(F32) + change).astype(BF16)


def shards(weights, warm_start):
    nrep, nsh = lax.axis_size("rep"), lax.axis_size("shard")
    _, rows, cols = weights.shape
    rank = warm_start.shape[2]
    half = rank // 2
    nown = math.gcd(cols // LANES, nsh)
    width = cols // nown
    dma = pltpu.SemaphoreType.DMA
    anyspace = pl.BlockSpec(memory_space=pl.ANY)
    vmem = pl.BlockSpec(memory_space=pltpu.VMEM)
    current, factors, bt = pl.pallas_call(
        functools.partial(comm_kernel, nrep, nsh, nown),
        out_shape=(
            jax.ShapeDtypeStruct((rows, cols), BF16),
            jax.ShapeDtypeStruct((STEPS, 2, half, cols), F32),
            jax.ShapeDtypeStruct((rows, LANES), BF16),
        ),
        in_specs=[anyspace, vmem],
        out_specs=(anyspace, anyspace, vmem),
        scratch_shapes=[
            pltpu.VMEM((rows, cols), BF16),
            pltpu.VMEM((STEPS, rank, rows), F32),
            pltpu.VMEM((STEPS, rank, rows), F32),
            pltpu.VMEM((STEPS, nsh, half, LANES), F32),
            pltpu.VMEM((STEPS, 2, half, cols), F32),
            pltpu.VMEM((STEPS, nown, half, width), F32),
            pltpu.VMEM((STEPS, nown, half, width), F32),
            pltpu.VMEM((STEPS, nsh, half, width), F32),
            pltpu.VMEM((STEPS, 2, half, cols), F32),
            pltpu.VMEM((STEPS, rows, LANES), BF16),
            dma((nown,)),
            dma((nown,)),
            dma((STEPS,)),
            dma((STEPS,)),
            dma((STEPS,)),
            dma((STEPS, nsh)),
            dma((STEPS, nsh)),
            dma((STEPS, nown)),
            dma((STEPS, nown)),
            dma((STEPS, nown)),
            dma((STEPS, nsh)),
            dma((STEPS, nsh)),
            dma((STEPS, nown)),
            dma((STEPS, nown)),
            dma((STEPS, nown)),
        ],
        compiler_params=pltpu.CompilerParams(
            collective_id=0, has_side_effects=True, vmem_limit_bytes=48 * 1024 * 1024
        ),
        name="rounds",
    )(weights[0], warm_start[0])
    factors = factors.reshape(STEPS, rank, cols)
    block = pl.BlockSpec((rows, width), lambda c: (0, c))
    corrected = pl.pallas_call(
        update_kernel,
        grid=(nown,),
        out_shape=jax.ShapeDtypeStruct((rows, cols), BF16),
        in_specs=[
            block,
            pl.BlockSpec((rows, LANES), lambda c: (0, 0)),
            pl.BlockSpec((None, rank, width), lambda c: (STEPS - 1, 0, c)),
        ],
        out_specs=block,
        name="update",
    )(current, bt, factors)
    return (corrected[None], factors[None])


def solution(mesh):
    placed = (P("rep", "shard", None), P("rep", None, None, None))
    return jax.shard_map(
        shards,
        mesh=mesh,
        in_specs=placed,
        out_specs=(P("rep", "shard", None), P("rep", None, None, None)),
        check_vma=False,
    )
```

```python
import functools
import math

import jax
import jax.numpy as jnp
from jax import lax
from jax.experimental import pallas as pl
from jax.experimental.pallas import tpu as pltpu
from jax.sharding import PartitionSpec as P

STEPS = 2
LANES = 128
VMEM = 67043328
F32 = jnp.float32
BF16 = jnp.bfloat16
NT = (((1,), (1,)), ((), ()))


def split(value):
    high = value.astype(BF16).astype(F32)
    return high, value - high


def stack_left(basis, scale):
    high, low = split(scale * basis)
    rank, rows = basis.shape
    pad = jnp.zeros((LANES - 3 * rank, rows), F32)
    return jnp.concatenate([high, high, low, pad], axis=0).T.astype(BF16)


def stack_right(factor):
    high, low = split(factor)
    rank, cols = factor.shape
    pad = jnp.zeros((LANES - 3 * rank, cols), F32)
    return jnp.concatenate([high, low, high, pad], axis=0).astype(BF16)


def whiten(gram, differ):
    rank = differ.shape[0]
    row = lax.broadcasted_iota(jnp.int32, (rank, 1), 0)
    pivots = jnp.ones((rank, 1), F32)
    for k in range(rank):
        pivot = gram[k : k + 1, k : k + 1]
        pivots = jnp.where(row == k, pivot, pivots)
        if k == rank - 1:
            break
        column = jnp.where(row > k, gram[:, k : k + 1] / pivot, 0.0)
        gram = gram - column * gram[k : k + 1, :]
        differ = differ - column * differ[k : k + 1, :]
    return differ / jnp.sqrt(pivots)


def comm_kernel(
    nrep, nsh, nown,
    w_hbm, starts_hbm, cur, fac, bt_out,
    starts, sk, skin, gbuf, pbuf, pin, psum, rsbuf, bt,
    ld_sem, wm_sem, sk_s, sk_r, g_s, g_r, p_s, p_r, rs_s, rs_r, ag_s, ag_r, fw_s, fw_r,
):
    rows, cols = cur.shape
    rank = starts.shape[1]
    half_rank = rank // 2
    width = cols // nown
    stride = nsh // nown
    half = nrep // 2
    me_r = lax.axis_index("rep")
    me_s = lax.axis_index("shard")
    me_j = me_s // stride
    bits = (me_r % 2, me_r // half)
    partners = (me_r + 1 - 2 * (me_r % 2), (me_r + half) % nrep)
    signs = tuple((1 - 2 * b).astype(F32) for b in bits)

    def where(j):
        return pl.ds(pl.multiple_of(j * width, LANES), width)

    def load(c):
        return pltpu.make_async_copy(
            w_hbm.at[:, pl.ds(c * width, width)], cur.at[:, pl.ds(c * width, width)], ld_sem.at[c]
        )

    def remote(src, dst, ssem, rsem, rep, shard):
        return pltpu.make_async_remote_copy(
            src_ref=src, dst_ref=dst, send_sem=ssem, recv_sem=rsem,
            device_id={"rep": rep, "shard": shard}, device_id_type=pl.DeviceIdType.MESH,
        )

    def owner(fn, negate=False):
        if stride == 1:
            if not negate:
                fn()
        else:
            here = me_s % stride != 0 if negate else me_s % stride == 0
            pl.when(here)(fn)

    warm = pltpu.make_async_copy(starts_hbm, starts, wm_sem)
    warm.start()
    for c in range(nown):
        load(c).start()

    barrier = pltpu.get_barrier_semaphore()
    for o in range(1, nsh):
        pl.semaphore_signal(
            barrier, inc=1, device_id={"rep": me_r, "shard": (me_s + o) % nsh},
            device_id_type=pl.DeviceIdType.MESH,
        )
    for p in partners:
        pl.semaphore_signal(
            barrier, inc=1, device_id={"rep": p, "shard": me_s},
            device_id_type=pl.DeviceIdType.MESH,
        )

    sketch = jnp.zeros((rank, rows), F32)
    warm.wait()
    for c in range(nown):
        load(c).wait()
        part = pl.ds(c * width, width)
        sketch = sketch + lax.dot_general(
            starts[0, :, part], cur[:, part], NT, preferred_element_type=F32
        )
    pl.semaphore_wait(barrier, nsh - 1 + 2)

    for k in range(STEPS):
        bit, mate, sign = bits[k], partners[k], signs[k]
        sk[k] = sketch
        swap = remote(sk.at[k], skin.at[k], sk_s.at[k], sk_r.at[k], mate, me_s)
        swap.start()
        swap.wait_recv()
        differ = sign * (sketch - skin[k])
        wide = jnp.concatenate([differ, jnp.zeros((LANES - rank, rows), F32)], axis=0)
        gram = lax.dot_general(
            differ, wide, NT, precision=lax.Precision.HIGHEST, preferred_element_type=F32
        )
        gbuf[k, me_s] = gram[:half_rank] + pltpu.roll(gram[half_rank:], rank, 1)

        def gsend(o):
            other = (me_s + o) % nsh
            return remote(
                gbuf.at[k, me_s], gbuf.at[k, me_s], g_s.at[k, other], g_r.at[k, me_s], me_r, other
            )

        def gwait(o):
            other = (me_s + o) % nsh
            return remote(
                gbuf.at[k, other], gbuf.at[k, other], g_s.at[k, other], g_r.at[k, other], me_r, other
            )

        for o in range(1, nsh):
            gsend(o).start()
        for o in range(1, nsh):
            gwait(o).wait_recv()
        total = gbuf[k, 0]
        for s in range(1, nsh):
            total = total + gbuf[k, s]
        gram = jnp.concatenate([total, pltpu.roll(total, LANES - rank, 1)], axis=0)
        basis = whiten(gram, differ)
        basis_half = basis.astype(BF16)

        def psend(j):
            return remote(
                pbuf.at[k, 1 - bit, :, where(j)], pin.at[k, j], p_s.at[k, j], p_r.at[k, j], mate, me_s
            )

        def rsend(j):
            return remote(
                psum.at[k, j], rsbuf.at[k, me_s], rs_s.at[k, j], rs_r.at[k, me_s], me_r, j * stride
            )

        def rwait(o):
            other = (me_s + o) % nsh
            return remote(
                rsbuf.at[k, other], rsbuf.at[k, other], rs_s.at[k, 0], rs_r.at[k, other], me_r, other
            )

        def asend(o):
            other = (me_s + o) % nsh
            piece = fac.at[k, bit, :, where(me_j)]
            return remote(piece, piece, ag_s.at[k, other], ag_r.at[k, me_j], me_r, other)

        def await_piece(j):
            piece = fac.at[k, bit, :, where(j)]
            return remote(piece, piece, ag_s.at[k, 0], ag_r.at[k, j], me_r, j * stride)

        def fsend(j):
            piece = fac.at[k, bit, :, where(j)]
            return remote(piece, piece, fw_s.at[k, j], fw_r.at[k, j], mate, me_s)

        def fwait(j):
            piece = fac.at[k, 1 - bit, :, where(j)]
            return remote(piece, piece, fw_s.at[k, j], fw_r.at[k, j], mate, me_s)

        order = [(me_j + 1 + i) % nown for i in range(nown)]

        def pass_on(i):
            j = order[i]
            psend(j).wait_recv()
            psum[k, j] = pbuf[k, bit, :, where(j)] + pin[k, j]
            if i < nown - 1:
                rsend(j).start()
            else:
                owner(lambda: rsend(j).start(), negate=True)

        lag = 2
        for i in range(nown):
            j = order[i]
            product = sign * jnp.dot(
                basis_half, cur[:, where(j)], preferred_element_type=F32
            )
            pbuf[k, 0, :, where(j)] = product[:half_rank]
            pbuf[k, 1, :, where(j)] = product[half_rank:]
            psend(j).start()
            if i >= lag:
                pass_on(i - lag)
        for i in range(max(nown - lag, 0), nown):
            pass_on(i)
        bt[k] = stack_left(basis, -0.5 * sign)

        def reduce_and_send():
            for o in range(1, nsh):
                rwait(o).wait_recv()
            total = psum[k, me_j]
            for o in range(1, nsh):
                total = total + rsbuf[k, (me_s + o) % nsh]
            fac[k, bit, :, where(me_j)] = total
            for o in range(1, nsh):
                asend(o).start()

        owner(reduce_and_send)
        owner(lambda: await_piece(me_j).wait_recv(), negate=True)
        fsend(me_j).start()
        if k + 1 < STEPS:
            sketch = jnp.zeros((rank, rows), F32)

        def take(i, sketch):
            j = (me_j + i) % nown
            fwait(j).wait_recv()
            if k + 1 == STEPS:
                return sketch
            piece = jnp.concatenate([fac[k, 0, :, where(j)], fac[k, 1, :, where(j)]], axis=0)
            change = jnp.dot(bt[k], stack_right(piece), preferred_element_type=F32)
            fresh = (cur[:, where(j)].astype(F32) + change).astype(BF16)
            cur[:, where(j)] = fresh
            return sketch + lax.dot_general(
                starts[k + 1, :, where(j)], fresh, NT, preferred_element_type=F32
            )

        for i in range(1, nown):
            j = (me_j + i) % nown
            await_piece(j).wait_recv()
            fsend(j).start()
            if i >= lag:
                sketch = take(i - lag, sketch)
        for i in range(max(nown - lag, 0), nown):
            sketch = take(i, sketch)

        swap.wait_send()
        for o in range(1, nsh):
            gsend(o).wait_send()
        for i in range(nown):
            psend(order[i]).wait_send()
            fsend(order[i]).wait_send()
            if i < nown - 1:
                rsend(order[i]).wait_send()
        owner(lambda: rsend(me_j).wait_send(), negate=True)

        def sent_all():
            for o in range(1, nsh):
                asend(o).wait_send()

        owner(sent_all)

    bt_out[...] = bt[STEPS - 1]


def update_kernel(cur, bt, fac, cur_out, fac_out, fresh, st_sem, fo_sem):
    pieces, _, width = fresh.shape
    factors = pltpu.make_async_copy(fac, fac_out, fo_sem)
    factors.start()

    def store(c):
        return pltpu.make_async_copy(
            fresh.at[c], cur_out.at[:, pl.ds(c * width, width)], st_sem.at[c]
        )

    for c in range(pieces):
        part = pl.ds(c * width, width)
        piece = jnp.concatenate([fac[STEPS - 1, 0, :, part], fac[STEPS - 1, 1, :, part]], axis=0)
        change = jnp.dot(bt[...], stack_right(piece), preferred_element_type=F32)
        fresh[c] = (cur[:, part].astype(F32) + change).astype(BF16)
        store(c).start()
    factors.wait()
    for c in range(pieces):
        store(c).wait()


def shards(weights, warm_start):
    nrep, nsh = lax.axis_size("rep"), lax.axis_size("shard")
    _, rows, cols = weights.shape
    rank = warm_start.shape[2]
    half = rank // 2
    nown = math.gcd(cols // LANES, nsh)
    width = cols // nown
    dma = pltpu.SemaphoreType.DMA
    held = 2 * rows * cols + 4 * STEPS * rank * cols + 2 * rows * LANES + 13000 * 1024
    hbm = pl.BlockSpec(memory_space=pltpu.HBM)
    vmem = pl.BlockSpec(memory_space=pltpu.VMEM)
    current, factors, bt = pl.pallas_call(
        functools.partial(comm_kernel, nrep, nsh, nown),
        out_shape=(
            jax.ShapeDtypeStruct((rows, cols), BF16),
            jax.ShapeDtypeStruct((STEPS, 2, half, cols), F32),
            jax.ShapeDtypeStruct((rows, LANES), BF16),
        ),
        in_specs=[hbm, hbm],
        out_specs=(vmem, vmem, vmem),
        scratch_shapes=[
            pltpu.VMEM(warm_start.shape[1:], BF16),
            pltpu.VMEM((STEPS, rank, rows), F32),
            pltpu.VMEM((STEPS, rank, rows), F32),
            pltpu.VMEM((STEPS, nsh, half, LANES), F32),
            pltpu.VMEM((STEPS, 2, half, cols), F32),
            pltpu.VMEM((STEPS, nown, half, width), F32),
            pltpu.VMEM((STEPS, nown, half, width), F32),
            pltpu.VMEM((STEPS, nsh, half, width), F32),
            pltpu.VMEM((STEPS, rows, LANES), BF16),
            dma((nown,)),
            dma,
            dma((STEPS,)),
            dma((STEPS,)),
            dma((STEPS, nsh)),
            dma((STEPS, nsh)),
            dma((STEPS, nown)),
            dma((STEPS, nown)),
            dma((STEPS, nown)),
            dma((STEPS, nsh)),
            dma((STEPS, nsh)),
            dma((STEPS, nown)),
            dma((STEPS, nown)),
            dma((STEPS, nown)),
        ],
        compiler_params=pltpu.CompilerParams(
            collective_id=0, has_side_effects=True, vmem_limit_bytes=VMEM - held
        ),
        name="rounds",
    )(weights[0], warm_start[0])
    corrected, factors = pl.pallas_call(
        update_kernel,
        out_shape=(
            jax.ShapeDtypeStruct((rows, cols), BF16),
            jax.ShapeDtypeStruct((STEPS, 2, half, cols), F32),
        ),
        in_specs=[vmem, vmem, vmem],
        out_specs=(hbm, hbm),
        scratch_shapes=[
            pltpu.VMEM((nown, rows, width), BF16),
            dma((nown,)),
            dma,
        ],
        compiler_params=pltpu.CompilerParams(vmem_limit_bytes=32 * 1024 * 1024),
        name="update",
    )(current, bt, factors)
    return (corrected[None], factors.reshape(1, STEPS, rank, cols))


def solution(mesh):
    placed = (P("rep", "shard", None), P("rep", None, None, None))
    return jax.shard_map(
        shards,
        mesh=mesh,
        in_specs=placed,
        out_specs=(P("rep", "shard", None), P("rep", None, None, None)),
        check_vma=False,
    )
```

```python
import functools
import math

import jax
import jax.numpy as jnp
from jax import lax
from jax.experimental import pallas as pl
from jax.experimental.pallas import tpu as pltpu
from jax.sharding import PartitionSpec as P

STEPS = 2
LANES = 128
VMEM = 67043328
F32 = jnp.float32
BF16 = jnp.bfloat16
NT = (((1,), (1,)), ((), ()))


def split(value):
    high = value.astype(BF16).astype(F32)
    return high, value - high


def stack_left(basis, scale):
    high, low = split(scale * basis)
    rank, rows = basis.shape
    pad = jnp.zeros((LANES - 3 * rank, rows), F32)
    return jnp.concatenate([high, high, low, pad], axis=0).T.astype(BF16)


def stack_right(factor):
    high, low = split(factor)
    rank, cols = factor.shape
    pad = jnp.zeros((LANES - 3 * rank, cols), F32)
    return jnp.concatenate([high, low, high, pad], axis=0).astype(BF16)


def whiten(gram, differ):
    rank = differ.shape[0]
    row = lax.broadcasted_iota(jnp.int32, (rank, 1), 0)
    pivots = jnp.ones((rank, 1), F32)
    for k in range(rank):
        pivot = gram[k : k + 1, k : k + 1]
        pivots = jnp.where(row == k, pivot, pivots)
        if k == rank - 1:
            break
        column = jnp.where(row > k, gram[:, k : k + 1] / pivot, 0.0)
        gram = gram - column * gram[k : k + 1, :]
        differ = differ - column * differ[k : k + 1, :]
    return differ / jnp.sqrt(pivots)


def comm_kernel(
    nrep, nsh, nown,
    w_hbm, starts_hbm, cur, fac, bt_out,
    starts, sk, skin, w1, w1in, cross, crossin, base, basein, gbuf, mbuf, pbuf, pin, psum, rsbuf, bt,
    ld_sem, wm_sem, sk_s, sk_r, w1_s, w1_r, cr_s, cr_r, ba_s, ba_r, g_s, g_r, m_s, m_r,
    p_s, p_r, rs_s, rs_r, ag_s, ag_r, fw_s, fw_r,
):
    rows, cols = cur.shape
    rank = starts.shape[1]
    half_rank = rank // 2
    width = cols // nown
    stride = nsh // nown
    half = nrep // 2
    me_r = lax.axis_index("rep")
    me_s = lax.axis_index("shard")
    me_j = me_s // stride
    bits = (me_r % 2, me_r // half)
    partners = (me_r + 1 - 2 * (me_r % 2), (me_r + half) % nrep)
    signs = tuple((1 - 2 * b).astype(F32) for b in bits)

    def where(j):
        return pl.ds(pl.multiple_of(j * width, LANES), width)

    def load(c):
        return pltpu.make_async_copy(
            w_hbm.at[:, pl.ds(c * width, width)], cur.at[:, pl.ds(c * width, width)], ld_sem.at[c]
        )

    def remote(src, dst, ssem, rsem, rep, shard):
        return pltpu.make_async_remote_copy(
            src_ref=src, dst_ref=dst, send_sem=ssem, recv_sem=rsem,
            device_id={"rep": rep, "shard": shard}, device_id_type=pl.DeviceIdType.MESH,
        )

    def owner(fn, negate=False):
        if stride == 1:
            if not negate:
                fn()
        else:
            here = me_s % stride != 0 if negate else me_s % stride == 0
            pl.when(here)(fn)

    warm = pltpu.make_async_copy(starts_hbm, starts, wm_sem)
    warm.start()
    for c in range(nown):
        load(c).start()

    mate, peer = partners
    barrier = pltpu.get_barrier_semaphore()

    def greet(rep, shard):
        pl.semaphore_signal(
            barrier, inc=1, device_id={"rep": rep, "shard": shard},
            device_id_type=pl.DeviceIdType.MESH,
        )

    for o in range(1, nsh):
        greet(me_r, (me_s + o) % nsh)
    for o in range(nsh):
        greet(peer, (me_s + o) % nsh)
    greet(mate, me_s)

    def pack(square):
        return square[:half_rank] + pltpu.roll(square[half_rank:], rank, 1)

    def unpack(tile):
        return jnp.concatenate([tile, pltpu.roll(tile, LANES - rank, 1)], axis=0)

    def padded(value):
        return jnp.concatenate([value, jnp.zeros((LANES - rank, rows), F32)], axis=0)

    def exact(a, b, dims):
        return lax.dot_general(
            a, b, dims, precision=lax.Precision.HIGHEST, preferred_element_type=F32
        )

    def slots(buf):
        total = buf[0]
        for s in range(1, nsh):
            total = total + buf[s]
        return total

    both = jnp.zeros((STEPS * rank, rows), F32)
    warm.wait()
    w1[...] = starts[1].astype(F32)
    for c in range(nown):
        load(c).wait()
        part = pl.ds(c * width, width)
        both = both + lax.dot_general(
            jnp.concatenate([starts[0, :, part], starts[1, :, part]], axis=0),
            cur[:, part], NT, preferred_element_type=F32,
        )
    sketches = (both[:rank], both[rank:])
    pl.semaphore_wait(barrier, 2 * nsh)

    def swap(k):
        return remote(sk.at[k], skin.at[k], sk_s.at[k], sk_r.at[k], partners[k], me_s)

    give_starts = remote(w1, w1in, w1_s, w1_r, mate, me_s)
    give_cross = remote(cross, crossin, cr_s, cr_r, mate, me_s)
    give_base = remote(base, basein, ba_s, ba_r, peer, me_s)
    for k in range(STEPS):
        sk[k] = sketches[k]
        swap(k).start()
    give_starts.start()

    def gsend(k, o):
        other = (me_s + o) % nsh
        return remote(
            gbuf.at[k, me_s], gbuf.at[k, me_s], g_s.at[k, other], g_r.at[k, me_s], me_r, other
        )

    def gwait(k, o):
        other = (me_s + o) % nsh
        return remote(
            gbuf.at[k, other], gbuf.at[k, other], g_s.at[k, other], g_r.at[k, other], me_r, other
        )

    def msend(g, o):
        other = (me_s + o) % nsh
        return remote(
            mbuf.at[0, me_s], mbuf.at[g, me_s], m_s.at[g, other], m_r.at[g, me_s],
            (me_r, peer)[g], other,
        )

    def mwait(g, o):
        other = (me_s + o) % nsh
        return remote(
            mbuf.at[g, other], mbuf.at[g, other], m_s.at[g, other], m_r.at[g, other],
            (me_r, peer)[g], other,
        )

    def psend(k, j):
        return remote(
            pbuf.at[k, 1 - bits[k], :, where(j)], pin.at[k, j], p_s.at[k, j], p_r.at[k, j],
            partners[k], me_s,
        )

    def rsend(k, j):
        return remote(
            psum.at[k, j], rsbuf.at[k, me_s], rs_s.at[k, j], rs_r.at[k, me_s], me_r, j * stride
        )

    def rwait(k, o):
        other = (me_s + o) % nsh
        return remote(
            rsbuf.at[k, other], rsbuf.at[k, other], rs_s.at[k, 0], rs_r.at[k, other], me_r, other
        )

    def asend(k, o):
        other = (me_s + o) % nsh
        piece = fac.at[k, bits[k], :, where(me_j)]
        return remote(piece, piece, ag_s.at[k, other], ag_r.at[k, me_j], me_r, other)

    def await_piece(k, j):
        piece = fac.at[k, bits[k], :, where(j)]
        return remote(piece, piece, ag_s.at[k, 0], ag_r.at[k, j], me_r, j * stride)

    def fsend(k, j):
        piece = fac.at[k, bits[k], :, where(j)]
        return remote(piece, piece, fw_s.at[k, j], fw_r.at[k, j], partners[k], me_s)

    def fwait(k, j):
        piece = fac.at[k, 1 - bits[k], :, where(j)]
        return remote(piece, piece, fw_s.at[k, j], fw_r.at[k, j], partners[k], me_s)

    order = [(me_j + 1 + i) % nown for i in range(nown)]

    def send_gram(k, differ):
        gbuf[k, me_s] = pack(exact(differ, padded(differ), NT))
        for o in range(1, nsh):
            gsend(k, o).start()

    def finish_basis(k, differ):
        for o in range(1, nsh):
            gwait(k, o).wait_recv()
        return whiten(unpack(slots(gbuf.at[k])), differ)

    def project(k, basis_half, j):
        product = signs[k] * jnp.dot(
            basis_half, cur[:, where(j)], preferred_element_type=F32
        )
        pbuf[k, 0, :, where(j)] = product[:half_rank]
        pbuf[k, 1, :, where(j)] = product[half_rank:]
        psend(k, j).start()

    def pass_on(k, j):
        psend(k, j).wait_recv()
        psum[k, j] = pbuf[k, bits[k], :, where(j)] + pin[k, j]

    def pass_out(k, i):
        pass_on(k, order[i])
        if i < nown - 1:
            rsend(k, order[i]).start()
        else:
            owner(lambda: rsend(k, order[i]).start(), negate=True)

    def reduce_and_send(k):
        def mine():
            for o in range(1, nsh):
                rwait(k, o).wait_recv()
            total = psum[k, me_j]
            for o in range(1, nsh):
                total = total + rsbuf[k, (me_s + o) % nsh]
            fac[k, bits[k], :, where(me_j)] = total
            for o in range(1, nsh):
                asend(k, o).start()

        owner(mine)

    def relay(k, i):
        j = (me_j + i) % nown
        if i:
            await_piece(k, j).wait_recv()
        else:
            owner(lambda: await_piece(k, j).wait_recv(), negate=True)
        fsend(k, j).start()

    lag = 2
    swap(0).wait_recv()
    differ = signs[0] * (sketches[0] - skin[0])
    send_gram(0, differ)
    give_starts.wait_recv()
    other = jnp.zeros((rank, rows), F32)
    for c in range(nown):
        part = pl.ds(c * width, width)
        other = other + lax.dot_general(
            w1in[:, part].astype(BF16), cur[:, part], NT, preferred_element_type=F32
        )
    cross[...] = other
    give_cross.start()
    basis = finish_basis(0, differ)
    base[...] = basis
    give_base.start()
    basis_half = basis.astype(BF16)
    give_cross.wait_recv()
    mbuf[0, me_s] = pack(
        signs[0] * exact(sketches[1] - crossin[...], padded(basis_half.astype(F32)), NT)
    )
    for o in range(nsh):
        if o:
            msend(0, o).start()
        msend(1, o).start()
    for i in range(nown):
        project(0, basis_half, order[i])
        if i >= lag:
            pass_out(0, i - lag)
    for i in range(max(nown - lag, 0), nown):
        pass_out(0, i)
    bt[0] = stack_left(basis, -0.5 * signs[0])
    swap(1).wait_recv()
    give_base.wait_recv()
    for o in range(nsh):
        if o:
            mwait(0, o).wait_recv()
        mwait(1, o).wait_recv()
    fix = -0.5 * signs[0]

    def moved(sketch, group, base_rows):
        return sketch + fix * exact(
            unpack(slots(mbuf.at[group])), padded(base_rows), (((1,), (0,)), ((), ()))
        )

    differ = signs[1] * (moved(sketches[1], 0, basis) - moved(skin[1], 1, basein[...]))
    send_gram(1, differ)
    reduce_and_send(0)
    basis = finish_basis(1, differ)
    basis_half = basis.astype(BF16)

    def update(i):
        j = (me_j + i) % nown
        fwait(0, j).wait_recv()
        piece = jnp.concatenate([fac[0, 0, :, where(j)], fac[0, 1, :, where(j)]], axis=0)
        change = jnp.dot(bt[0], stack_right(piece), preferred_element_type=F32)
        cur[:, where(j)] = (cur[:, where(j)].astype(F32) + change).astype(BF16)
        project(1, basis_half, j)

    seq = list(range(1, nown)) + [0]
    relay(0, 0)
    for n in range(1, nown):
        relay(0, n)
    bt_out[...] = stack_left(basis, -0.5 * signs[1])
    for n in range(nown):
        update(seq[n])
        if n >= lag:
            pass_out(1, n - lag)
    for i in range(max(nown - lag, 0), nown):
        pass_out(1, i)
    reduce_and_send(1)
    for n in range(nown):
        relay(1, n)
    for n in range(nown):
        fwait(1, (me_j + n) % nown).wait_recv()

    give_starts.wait_send()
    give_cross.wait_send()
    give_base.wait_send()
    for o in range(nsh):
        if o:
            msend(0, o).wait_send()
        msend(1, o).wait_send()
    for k in range(STEPS):
        swap(k).wait_send()
        for o in range(1, nsh):
            gsend(k, o).wait_send()
        for i in range(nown):
            psend(k, order[i]).wait_send()
            fsend(k, order[i]).wait_send()
            if i < nown - 1:
                rsend(k, order[i]).wait_send()

    def sent_all():
        for k in range(STEPS):
            for o in range(1, nsh):
                asend(k, o).wait_send()

    def sent_own():
        for k in range(STEPS):
            rsend(k, me_j).wait_send()

    owner(sent_all)
    owner(sent_own, negate=True)


def update_kernel(cur, bt, fac, cur_out, fac_out, fresh, st_sem, fo_sem):
    pieces, _, width = fresh.shape
    factors = pltpu.make_async_copy(fac, fac_out, fo_sem)
    factors.start()

    def store(c):
        return pltpu.make_async_copy(
            fresh.at[c], cur_out.at[:, pl.ds(c * width, width)], st_sem.at[c]
        )

    for c in range(pieces):
        part = pl.ds(c * width, width)
        piece = jnp.concatenate([fac[STEPS - 1, 0, :, part], fac[STEPS - 1, 1, :, part]], axis=0)
        change = jnp.dot(bt[...], stack_right(piece), preferred_element_type=F32)
        fresh[c] = (cur[:, part].astype(F32) + change).astype(BF16)
        store(c).start()
    factors.wait()
    for c in range(pieces):
        store(c).wait()


def shards(weights, warm_start):
    nrep, nsh = lax.axis_size("rep"), lax.axis_size("shard")
    _, rows, cols = weights.shape
    rank = warm_start.shape[2]
    half = rank // 2
    nown = math.gcd(cols // LANES, nsh)
    width = cols // nown
    dma = pltpu.SemaphoreType.DMA
    held = 2 * rows * cols + 4 * STEPS * rank * cols + 2 * rows * LANES + 13000 * 1024
    hbm = pl.BlockSpec(memory_space=pltpu.HBM)
    vmem = pl.BlockSpec(memory_space=pltpu.VMEM)
    current, factors, bt = pl.pallas_call(
        functools.partial(comm_kernel, nrep, nsh, nown),
        out_shape=(
            jax.ShapeDtypeStruct((rows, cols), BF16),
            jax.ShapeDtypeStruct((STEPS, 2, half, cols), F32),
            jax.ShapeDtypeStruct((rows, LANES), BF16),
        ),
        in_specs=[hbm, hbm],
        out_specs=(vmem, vmem, vmem),
        scratch_shapes=[
            pltpu.VMEM(warm_start.shape[1:], BF16),
            pltpu.VMEM((STEPS, rank, rows), F32),
            pltpu.VMEM((STEPS, rank, rows), F32),
            pltpu.VMEM((rank, cols), F32),
            pltpu.VMEM((rank, cols), F32),
            pltpu.VMEM((rank, rows), F32),
            pltpu.VMEM((rank, rows), F32),
            pltpu.VMEM((rank, rows), F32),
            pltpu.VMEM((rank, rows), F32),
            pltpu.VMEM((STEPS, nsh, half, LANES), F32),
            pltpu.VMEM((STEPS, nsh, half, LANES), F32),
            pltpu.VMEM((STEPS, 2, half, cols), F32),
            pltpu.VMEM((STEPS, nown, half, width), F32),
            pltpu.VMEM((STEPS, nown, half, width), F32),
            pltpu.VMEM((STEPS, nsh, half, width), F32),
            pltpu.VMEM((1, rows, LANES), BF16),
            dma((nown,)),
            dma,
            dma((STEPS,)),
            dma((STEPS,)),
            dma,
            dma,
            dma,
            dma,
            dma,
            dma,
            dma((STEPS, nsh)),
            dma((STEPS, nsh)),
            dma((STEPS, nsh)),
            dma((STEPS, nsh)),
            dma((STEPS, nown)),
            dma((STEPS, nown)),
            dma((STEPS, nown)),
            dma((STEPS, nsh)),
            dma((STEPS, nsh)),
            dma((STEPS, nown)),
            dma((STEPS, nown)),
            dma((STEPS, nown)),
        ],
        compiler_params=pltpu.CompilerParams(
            collective_id=0, has_side_effects=True, vmem_limit_bytes=VMEM - held
        ),
        name="rounds",
    )(weights[0], warm_start[0])
    corrected, factors = pl.pallas_call(
        update_kernel,
        out_shape=(
            jax.ShapeDtypeStruct((rows, cols), BF16),
            jax.ShapeDtypeStruct((STEPS, 2, half, cols), F32),
        ),
        in_specs=[vmem, vmem, vmem],
        out_specs=(hbm, hbm),
        scratch_shapes=[
            pltpu.VMEM((nown, rows, width), BF16),
            dma((nown,)),
            dma,
        ],
        compiler_params=pltpu.CompilerParams(vmem_limit_bytes=32 * 1024 * 1024),
        name="update",
    )(current, bt, factors)
    return (corrected[None], factors.reshape(1, STEPS, rank, cols))


def solution(mesh):
    placed = (P("rep", "shard", None), P("rep", None, None, None))
    return jax.shard_map(
        shards,
        mesh=mesh,
        in_specs=placed,
        out_specs=(P("rep", "shard", None), P("rep", None, None, None)),
        check_vma=False,
    )
```

```python
import functools
import math

import jax
import jax.numpy as jnp
from jax import lax
from jax.experimental import pallas as pl
from jax.experimental.pallas import tpu as pltpu
from jax.sharding import PartitionSpec as P

STEPS = 2
LANES = 128
VMEM = 67043328
F32 = jnp.float32
BF16 = jnp.bfloat16
NT = (((1,), (1,)), ((), ()))


def split(value):
    high = value.astype(BF16).astype(F32)
    return high, value - high


def stack_left(basis, scale):
    high, low = split(scale * basis)
    rank, rows = basis.shape
    pad = jnp.zeros((LANES - 3 * rank, rows), F32)
    return jnp.concatenate([high, high, low, pad], axis=0).T.astype(BF16)


def stack_right(factor):
    high, low = split(factor)
    rank, cols = factor.shape
    pad = jnp.zeros((LANES - 3 * rank, cols), F32)
    return jnp.concatenate([high, low, high, pad], axis=0).astype(BF16)


def whiten(gram, differ):
    rank = differ.shape[0]
    row = lax.broadcasted_iota(jnp.int32, (rank, 1), 0)
    pivots = jnp.ones((rank, 1), F32)
    for k in range(rank):
        pivot = gram[k : k + 1, k : k + 1]
        pivots = jnp.where(row == k, pivot, pivots)
        if k == rank - 1:
            break
        column = jnp.where(row > k, gram[:, k : k + 1] / pivot, 0.0)
        gram = gram - column * gram[k : k + 1, :]
        differ = differ - column * differ[k : k + 1, :]
    return differ / jnp.sqrt(pivots)


def comm_kernel(
    nrep, nsh, nown,
    w_hbm, starts_hbm, cur, fac, bt_out,
    starts, sk, skin, w1, w1in, cross, crossin, base, basein, gbuf, mbuf, qbuf, peerfac, pbuf, pin, psum, rsbuf, bt,
    ld_sem, wm_sem, sk_s, sk_r, w1_s, w1_r, cr_s, cr_r, ba_s, ba_r, g_s, g_r, m_s, m_r, q_s, q_r, pf_s, pf_r,
    p_s, p_r, rs_s, rs_r, ag_s, ag_r, fw_s, fw_r,
):
    rows, cols = cur.shape
    rank = starts.shape[1]
    half_rank = rank // 2
    width = cols // nown
    stride = nsh // nown
    half = nrep // 2
    me_r = lax.axis_index("rep")
    me_s = lax.axis_index("shard")
    me_j = me_s // stride
    bits = (me_r % 2, me_r // half)
    partners = (me_r + 1 - 2 * (me_r % 2), (me_r + half) % nrep)
    signs = tuple((1 - 2 * b).astype(F32) for b in bits)

    def where(j):
        return pl.ds(pl.multiple_of(j * width, LANES), width)

    def load(c):
        return pltpu.make_async_copy(
            w_hbm.at[:, pl.ds(c * width, width)], cur.at[:, pl.ds(c * width, width)], ld_sem.at[c]
        )

    def remote(src, dst, ssem, rsem, rep, shard):
        return pltpu.make_async_remote_copy(
            src_ref=src, dst_ref=dst, send_sem=ssem, recv_sem=rsem,
            device_id={"rep": rep, "shard": shard}, device_id_type=pl.DeviceIdType.MESH,
        )

    def owner(fn, negate=False):
        if stride == 1:
            if not negate:
                fn()
        else:
            here = me_s % stride != 0 if negate else me_s % stride == 0
            pl.when(here)(fn)

    warm = pltpu.make_async_copy(starts_hbm, starts, wm_sem)
    warm.start()
    for c in range(nown):
        load(c).start()

    mate, peer = partners
    barrier = pltpu.get_barrier_semaphore()

    def greet(rep, shard):
        pl.semaphore_signal(
            barrier, inc=1, device_id={"rep": rep, "shard": shard},
            device_id_type=pl.DeviceIdType.MESH,
        )

    for o in range(1, nsh):
        greet(me_r, (me_s + o) % nsh)
    for o in range(nsh):
        greet(peer, (me_s + o) % nsh)
    greet(mate, me_s)

    def pack(square):
        return square[:half_rank] + pltpu.roll(square[half_rank:], rank, 1)

    def unpack(tile):
        return jnp.concatenate([tile, pltpu.roll(tile, LANES - rank, 1)], axis=0)

    def padded(value):
        return jnp.concatenate([value, jnp.zeros((LANES - rank, rows), F32)], axis=0)

    def exact(a, b, dims):
        return lax.dot_general(
            a, b, dims, precision=lax.Precision.HIGHEST, preferred_element_type=F32
        )

    def slots(buf):
        total = buf[0]
        for s in range(1, nsh):
            total = total + buf[s]
        return total

    both = jnp.zeros((STEPS * rank, rows), F32)
    warm.wait()
    w1[...] = starts[1].astype(F32)
    for c in range(nown):
        load(c).wait()
        part = pl.ds(c * width, width)
        both = both + lax.dot_general(
            jnp.concatenate([starts[0, :, part], starts[1, :, part]], axis=0),
            cur[:, part], NT, preferred_element_type=F32,
        )
    sketches = (both[:rank], both[rank:])
    pl.semaphore_wait(barrier, 2 * nsh)

    def swap(k):
        return remote(sk.at[k], skin.at[k], sk_s.at[k], sk_r.at[k], partners[k], me_s)

    give_starts = remote(w1, w1in, w1_s, w1_r, mate, me_s)
    give_cross = remote(cross, crossin, cr_s, cr_r, mate, me_s)
    give_base = remote(base, basein, ba_s, ba_r, peer, me_s)
    for k in range(STEPS):
        sk[k] = sketches[k]
        swap(k).start()
    give_starts.start()

    def gsend(k, o):
        other = (me_s + o) % nsh
        return remote(
            gbuf.at[k, me_s], gbuf.at[k, me_s], g_s.at[k, other], g_r.at[k, me_s], me_r, other
        )

    def gwait(k, o):
        other = (me_s + o) % nsh
        return remote(
            gbuf.at[k, other], gbuf.at[k, other], g_s.at[k, other], g_r.at[k, other], me_r, other
        )

    def small(buf, ssem, rsem):
        def send(g, o):
            other = (me_s + o) % nsh
            return remote(
                buf.at[0, me_s], buf.at[g, me_s], ssem.at[g, other], rsem.at[g, me_s],
                (me_r, peer)[g], other,
            )

        def arrival(g, o):
            other = (me_s + o) % nsh
            return remote(
                buf.at[g, other], buf.at[g, other], ssem.at[g, other], rsem.at[g, other],
                (me_r, peer)[g], other,
            )

        return send, arrival

    pairs = [(g, o) for o in range(nsh) for g in range(2) if g or o]
    msend, mwait = small(mbuf, m_s, m_r)
    qsend, qwait = small(qbuf, q_s, q_r)

    def psend(k, j):
        return remote(
            pbuf.at[k, 1 - bits[k], :, where(j)], pin.at[k, j], p_s.at[k, j], p_r.at[k, j],
            partners[k], me_s,
        )

    def rsend(k, j):
        return remote(
            psum.at[k, j], rsbuf.at[k, me_s], rs_s.at[k, j], rs_r.at[k, me_s], me_r, j * stride
        )

    def rwait(k, o):
        other = (me_s + o) % nsh
        return remote(
            rsbuf.at[k, other], rsbuf.at[k, other], rs_s.at[k, 0], rs_r.at[k, other], me_r, other
        )

    def asend(k, o):
        other = (me_s + o) % nsh
        piece = fac.at[k, bits[k], :, where(me_j)]
        return remote(piece, piece, ag_s.at[k, other], ag_r.at[k, me_j], me_r, other)

    def await_piece(k, j):
        piece = fac.at[k, bits[k], :, where(j)]
        return remote(piece, piece, ag_s.at[k, 0], ag_r.at[k, j], me_r, j * stride)

    def fsend(k, j):
        piece = fac.at[k, bits[k], :, where(j)]
        return remote(piece, piece, fw_s.at[k, j], fw_r.at[k, j], partners[k], me_s)

    def fwait(k, j):
        piece = fac.at[k, 1 - bits[k], :, where(j)]
        return remote(piece, piece, fw_s.at[k, j], fw_r.at[k, j], partners[k], me_s)

    order = [(me_j + 1 + i) % nown for i in range(nown)]

    def send_gram(k, differ):
        gbuf[k, me_s] = pack(exact(differ, padded(differ), NT))
        for o in range(1, nsh):
            gsend(k, o).start()

    def finish_basis(k, differ):
        for o in range(1, nsh):
            gwait(k, o).wait_recv()
        return whiten(unpack(slots(gbuf.at[k])), differ)

    def project(k, basis_half, j):
        product = signs[k] * jnp.dot(
            basis_half, cur[:, where(j)], preferred_element_type=F32
        )
        pbuf[k, 0, :, where(j)] = product[:half_rank]
        pbuf[k, 1, :, where(j)] = product[half_rank:]
        psend(k, j).start()

    def pass_on(k, j):
        psend(k, j).wait_recv()
        psum[k, j] = pbuf[k, bits[k], :, where(j)] + pin[k, j]

    def pass_out(k, i):
        pass_on(k, order[i])
        if i < nown - 1:
            rsend(k, order[i]).start()
        else:
            owner(lambda: rsend(k, order[i]).start(), negate=True)

    def reduce_and_send(k, extra=None):
        def mine():
            for o in range(1, nsh):
                rwait(k, o).wait_recv()
            total = psum[k, me_j]
            for o in range(1, nsh):
                total = total + rsbuf[k, (me_s + o) % nsh]
            if extra is not None:
                total = total + extra
            fac[k, bits[k], :, where(me_j)] = total
            for o in range(nsh - 1, 0, -1):
                asend(k, o).start()

        owner(mine)

    def relay(k, i):
        j = (me_j + i) % nown
        if i:
            await_piece(k, j).wait_recv()
        else:
            owner(lambda: await_piece(k, j).wait_recv(), negate=True)
        fsend(k, j).start()

    lag = 2
    swap(0).wait_recv()
    differ = signs[0] * (sketches[0] - skin[0])
    send_gram(0, differ)
    give_starts.wait_recv()
    other = jnp.zeros((rank, rows), F32)
    for c in range(nown):
        part = pl.ds(c * width, width)
        other = other + lax.dot_general(
            w1in[:, part].astype(BF16), cur[:, part], NT, preferred_element_type=F32
        )
    cross[...] = other
    give_cross.start()
    basis = finish_basis(0, differ)
    base[...] = basis
    give_base.start()
    basis_half = basis.astype(BF16)
    give_cross.wait_recv()
    mbuf[0, me_s] = pack(
        signs[0] * exact(sketches[1] - crossin[...], padded(basis_half.astype(F32)), NT)
    )
    for g, o in pairs:
        msend(g, o).start()
    for i in range(nown):
        project(0, basis_half, order[i])
        if i >= lag:
            pass_out(0, i - lag)
    for i in range(max(nown - lag, 0), nown):
        pass_out(0, i)
    bt[0] = stack_left(basis, -0.5 * signs[0])
    swap(1).wait_recv()
    give_base.wait_recv()
    for g, o in pairs:
        mwait(g, o).wait_recv()
    fix = -0.5 * signs[0]

    def moved(sketch, group, base_rows):
        return sketch + fix * exact(
            unpack(slots(mbuf.at[group])), padded(base_rows), (((1,), (0,)), ((), ()))
        )

    differ = signs[1] * (moved(sketches[1], 0, basis) - moved(skin[1], 1, basein[...]))
    send_gram(1, differ)
    reduce_and_send(0)
    relay(0, 0)
    basis = finish_basis(1, differ)
    basis_half = basis.astype(BF16)
    qbuf[0, me_s] = pack(exact(basis_half.astype(F32), padded(base[...]), NT))
    for g, o in pairs:
        qsend(g, o).start()
    for i in range(nown):
        project(1, basis_half, order[i])
        if i >= lag:
            pass_out(1, i - lag)
    for i in range(max(nown - lag, 0), nown):
        pass_out(1, i)
    for n in range(1, nown):
        relay(0, n)
    fwait(0, me_j).wait_recv()
    give_factor = remote(
        fac.at[0, :, :, where(me_j)], peerfac, pf_s, pf_r, peer, me_s
    )
    give_factor.start()
    bt_out[...] = stack_left(basis, -0.5 * signs[1])

    def update(j):
        piece = jnp.concatenate([fac[0, 0, :, where(j)], fac[0, 1, :, where(j)]], axis=0)
        change = jnp.dot(bt[0], stack_right(piece), preferred_element_type=F32)
        cur[:, where(j)] = (cur[:, where(j)].astype(F32) + change).astype(BF16)

    update(me_j)
    for n in range(1, nown):
        j = (me_j + n) % nown
        fwait(0, j).wait_recv()
        update(j)
    for g, o in pairs:
        qwait(g, o).wait_recv()
    give_factor.wait_recv()

    def shift(group, halves):
        piece = jnp.concatenate(
            [halves[0], halves[1], jnp.zeros((LANES - rank, width), F32)], axis=0
        )
        return exact(unpack(slots(qbuf.at[group])), piece, (((1,), (0,)), ((), ())))

    own = (fac[0, 0, :, where(me_j)], fac[0, 1, :, where(me_j)])
    shifted = fix * signs[1] * (shift(0, own) - shift(1, (peerfac[0], peerfac[1])))
    reduce_and_send(1, jnp.where(bits[1] == 0, shifted[:half_rank], shifted[half_rank:]))
    for n in range(nown):
        relay(1, n)
    for n in range(nown):
        fwait(1, (me_j + n) % nown).wait_recv()

    give_starts.wait_send()
    give_cross.wait_send()
    give_base.wait_send()
    give_factor.wait_send()
    for g, o in pairs:
        msend(g, o).wait_send()
        qsend(g, o).wait_send()
    for k in range(STEPS):
        swap(k).wait_send()
        for o in range(1, nsh):
            gsend(k, o).wait_send()
        for i in range(nown):
            psend(k, order[i]).wait_send()
            fsend(k, order[i]).wait_send()
            if i < nown - 1:
                rsend(k, order[i]).wait_send()

    def sent_all():
        for k in range(STEPS):
            for o in range(1, nsh):
                asend(k, o).wait_send()

    def sent_own():
        for k in range(STEPS):
            rsend(k, me_j).wait_send()

    owner(sent_all)
    owner(sent_own, negate=True)


def update_kernel(cur, bt, fac, cur_out, fac_out, fresh, st_sem, fo_sem):
    pieces, _, width = fresh.shape
    factors = pltpu.make_async_copy(fac, fac_out, fo_sem)
    factors.start()

    def store(c):
        return pltpu.make_async_copy(
            fresh.at[c], cur_out.at[:, pl.ds(c * width, width)], st_sem.at[c]
        )

    for c in range(pieces):
        part = pl.ds(c * width, width)
        piece = jnp.concatenate([fac[STEPS - 1, 0, :, part], fac[STEPS - 1, 1, :, part]], axis=0)
        change = jnp.dot(bt[...], stack_right(piece), preferred_element_type=F32)
        fresh[c] = (cur[:, part].astype(F32) + change).astype(BF16)
        store(c).start()
    factors.wait()
    for c in range(pieces):
        store(c).wait()


def shards(weights, warm_start):
    nrep, nsh = lax.axis_size("rep"), lax.axis_size("shard")
    _, rows, cols = weights.shape
    rank = warm_start.shape[2]
    half = rank // 2
    nown = math.gcd(cols // LANES, nsh)
    width = cols // nown
    dma = pltpu.SemaphoreType.DMA
    held = 2 * rows * cols + 4 * STEPS * rank * cols + 2 * rows * LANES + 13000 * 1024
    hbm = pl.BlockSpec(memory_space=pltpu.HBM)
    vmem = pl.BlockSpec(memory_space=pltpu.VMEM)
    current, factors, bt = pl.pallas_call(
        functools.partial(comm_kernel, nrep, nsh, nown),
        out_shape=(
            jax.ShapeDtypeStruct((rows, cols), BF16),
            jax.ShapeDtypeStruct((STEPS, 2, half, cols), F32),
            jax.ShapeDtypeStruct((rows, LANES), BF16),
        ),
        in_specs=[hbm, hbm],
        out_specs=(vmem, vmem, vmem),
        scratch_shapes=[
            pltpu.VMEM(warm_start.shape[1:], BF16),
            pltpu.VMEM((STEPS, rank, rows), F32),
            pltpu.VMEM((STEPS, rank, rows), F32),
            pltpu.VMEM((rank, cols), F32),
            pltpu.VMEM((rank, cols), F32),
            pltpu.VMEM((rank, rows), F32),
            pltpu.VMEM((rank, rows), F32),
            pltpu.VMEM((rank, rows), F32),
            pltpu.VMEM((rank, rows), F32),
            pltpu.VMEM((STEPS, nsh, half, LANES), F32),
            pltpu.VMEM((2, nsh, half, LANES), F32),
            pltpu.VMEM((2, nsh, half, LANES), F32),
            pltpu.VMEM((2, half, width), F32),
            pltpu.VMEM((STEPS, 2, half, cols), F32),
            pltpu.VMEM((STEPS, nown, half, width), F32),
            pltpu.VMEM((STEPS, nown, half, width), F32),
            pltpu.VMEM((STEPS, nsh, half, width), F32),
            pltpu.VMEM((1, rows, LANES), BF16),
            dma((nown,)),
            dma,
            dma((STEPS,)),
            dma((STEPS,)),
            dma,
            dma,
            dma,
            dma,
            dma,
            dma,
            dma((STEPS, nsh)),
            dma((STEPS, nsh)),
            dma((2, nsh)),
            dma((2, nsh)),
            dma((2, nsh)),
            dma((2, nsh)),
            dma,
            dma,
            dma((STEPS, nown)),
            dma((STEPS, nown)),
            dma((STEPS, nown)),
            dma((STEPS, nsh)),
            dma((STEPS, nsh)),
            dma((STEPS, nown)),
            dma((STEPS, nown)),
            dma((STEPS, nown)),
        ],
        compiler_params=pltpu.CompilerParams(
            collective_id=0, has_side_effects=True, vmem_limit_bytes=VMEM - held
        ),
        name="rounds",
    )(weights[0], warm_start[0])
    corrected, factors = pl.pallas_call(
        update_kernel,
        out_shape=(
            jax.ShapeDtypeStruct((rows, cols), BF16),
            jax.ShapeDtypeStruct((STEPS, 2, half, cols), F32),
        ),
        in_specs=[vmem, vmem, vmem],
        out_specs=(hbm, hbm),
        scratch_shapes=[
            pltpu.VMEM((nown, rows, width), BF16),
            dma((nown,)),
            dma,
        ],
        compiler_params=pltpu.CompilerParams(vmem_limit_bytes=32 * 1024 * 1024),
        name="update",
    )(current, bt, factors)
    return (corrected[None], factors.reshape(1, STEPS, rank, cols))


def solution(mesh):
    placed = (P("rep", "shard", None), P("rep", None, None, None))
    return jax.shard_map(
        shards,
        mesh=mesh,
        in_specs=placed,
        out_specs=(P("rep", "shard", None), P("rep", None, None, None)),
        check_vma=False,
    )
```

```python
import functools
import math

import jax
import jax.numpy as jnp
from jax import lax
from jax.experimental import pallas as pl
from jax.experimental.pallas import tpu as pltpu
from jax.sharding import PartitionSpec as P

STEPS = 2
LANES = 128
VMEM = 67043328
F32 = jnp.float32
BF16 = jnp.bfloat16
NT = (((1,), (1,)), ((), ()))


def split(value):
    high = value.astype(BF16).astype(F32)
    return high, value - high


def stack_left(basis, scale):
    high, low = split(scale * basis)
    rank, rows = basis.shape
    pad = jnp.zeros((LANES - 3 * rank, rows), F32)
    return jnp.concatenate([high, high, low, pad], axis=0).T.astype(BF16)


def stack_right(factor):
    high, low = split(factor)
    rank, cols = factor.shape
    pad = jnp.zeros((LANES - 3 * rank, cols), F32)
    return jnp.concatenate([high, low, high, pad], axis=0).astype(BF16)


def whiten(gram, differ):
    rank = differ.shape[0]
    row = lax.broadcasted_iota(jnp.int32, (rank, 1), 0)
    pivots = jnp.ones((rank, 1), F32)
    for k in range(rank):
        pivot = gram[k : k + 1, k : k + 1]
        pivots = jnp.where(row == k, pivot, pivots)
        if k == rank - 1:
            break
        column = jnp.where(row > k, gram[:, k : k + 1] / pivot, 0.0)
        gram = gram - column * gram[k : k + 1, :]
        differ = differ - column * differ[k : k + 1, :]
    return differ / jnp.sqrt(pivots)


def comm_kernel(
    nrep, nsh, nown,
    w_hbm, starts_hbm, cur, fac, bt_out,
    starts, sk, skin, w1, w1in, cross, crossin, base, basein, gbuf, mbuf, pbuf, pin, psum, rsbuf, bt,
    ld_sem, wm_sem, sk_s, sk_r, w1_s, w1_r, cr_s, cr_r, ba_s, ba_r, g_s, g_r, m_s, m_r,
    p_s, p_r, rs_s, rs_r, ag_s, ag_r, fw_s, fw_r,
):
    rows, cols = cur.shape
    rank = starts.shape[1]
    half_rank = rank // 2
    width = cols // nown
    stride = nsh // nown
    half = nrep // 2
    me_r = lax.axis_index("rep")
    me_s = lax.axis_index("shard")
    me_j = me_s // stride
    bits = (me_r % 2, me_r // half)
    partners = (me_r + 1 - 2 * (me_r % 2), (me_r + half) % nrep)
    signs = tuple((1 - 2 * b).astype(F32) for b in bits)

    def where(j):
        return pl.ds(pl.multiple_of(j * width, LANES), width)

    def load(c):
        return pltpu.make_async_copy(
            w_hbm.at[:, pl.ds(c * width, width)], cur.at[:, pl.ds(c * width, width)], ld_sem.at[c]
        )

    def remote(src, dst, ssem, rsem, rep, shard):
        return pltpu.make_async_remote_copy(
            src_ref=src, dst_ref=dst, send_sem=ssem, recv_sem=rsem,
            device_id={"rep": rep, "shard": shard}, device_id_type=pl.DeviceIdType.MESH,
        )

    def owner(fn, negate=False):
        if stride == 1:
            if not negate:
                fn()
        else:
            here = me_s % stride != 0 if negate else me_s % stride == 0
            pl.when(here)(fn)

    warm = pltpu.make_async_copy(starts_hbm, starts, wm_sem)
    warm.start()
    for c in range(nown):
        load(c).start()

    mate, peer = partners
    barrier = pltpu.get_barrier_semaphore()

    def greet(rep, shard):
        pl.semaphore_signal(
            barrier, inc=1, device_id={"rep": rep, "shard": shard},
            device_id_type=pl.DeviceIdType.MESH,
        )

    for o in range(1, nsh):
        greet(me_r, (me_s + o) % nsh)
    for o in range(nsh):
        greet(peer, (me_s + o) % nsh)
    greet(mate, me_s)

    def pack(square):
        return square[:half_rank] + pltpu.roll(square[half_rank:], rank, 1)

    def unpack(tile):
        return jnp.concatenate([tile, pltpu.roll(tile, LANES - rank, 1)], axis=0)

    def padded(value):
        return jnp.concatenate([value, jnp.zeros((LANES - rank, rows), F32)], axis=0)

    def exact(a, b, dims):
        return lax.dot_general(
            a, b, dims, precision=lax.Precision.HIGHEST, preferred_element_type=F32
        )

    def slots(buf):
        total = buf[0]
        for s in range(1, nsh):
            total = total + buf[s]
        return total

    both = jnp.zeros((STEPS * rank, rows), F32)
    warm.wait()
    w1[...] = starts[1].astype(F32)
    for c in range(nown):
        load(c).wait()
        part = pl.ds(c * width, width)
        both = both + lax.dot_general(
            jnp.concatenate([starts[0, :, part], starts[1, :, part]], axis=0),
            cur[:, part], NT, preferred_element_type=F32,
        )
    sketches = (both[:rank], both[rank:])
    pl.semaphore_wait(barrier, 2 * nsh)

    def swap(k):
        return remote(sk.at[k], skin.at[k], sk_s.at[k], sk_r.at[k], partners[k], me_s)

    give_starts = remote(w1, w1in, w1_s, w1_r, mate, me_s)
    give_cross = remote(cross, crossin, cr_s, cr_r, mate, me_s)
    give_base = remote(base, basein, ba_s, ba_r, peer, me_s)
    for k in range(STEPS):
        sk[k] = sketches[k]
        swap(k).start()
    give_starts.start()

    def gsend(k, o):
        other = (me_s + o) % nsh
        return remote(
            gbuf.at[k, me_s], gbuf.at[k, me_s], g_s.at[k, other], g_r.at[k, me_s], me_r, other
        )

    def gwait(k, o):
        other = (me_s + o) % nsh
        return remote(
            gbuf.at[k, other], gbuf.at[k, other], g_s.at[k, other], g_r.at[k, other], me_r, other
        )

    def msend(g, o):
        other = (me_s + o) % nsh
        return remote(
            mbuf.at[0, me_s], mbuf.at[g, me_s], m_s.at[g, other], m_r.at[g, me_s],
            (me_r, peer)[g], other,
        )

    def mwait(g, o):
        other = (me_s + o) % nsh
        return remote(
            mbuf.at[g, other], mbuf.at[g, other], m_s.at[g, other], m_r.at[g, other],
            (me_r, peer)[g], other,
        )

    def psend(k, j):
        return remote(
            pbuf.at[k, 1 - bits[k], :, where(j)], pin.at[k, j], p_s.at[k, j], p_r.at[k, j],
            partners[k], me_s,
        )

    def rsend(k, j):
        return remote(
            psum.at[k, j], rsbuf.at[k, me_s], rs_s.at[k, j], rs_r.at[k, me_s], me_r, j * stride
        )

    def rwait(k, o):
        other = (me_s + o) % nsh
        return remote(
            rsbuf.at[k, other], rsbuf.at[k, other], rs_s.at[k, 0], rs_r.at[k, other], me_r, other
        )

    def asend(k, o):
        other = (me_s + o) % nsh
        piece = fac.at[k, bits[k], :, where(me_j)]
        return remote(piece, piece, ag_s.at[k, other], ag_r.at[k, me_j], me_r, other)

    def await_piece(k, j):
        piece = fac.at[k, bits[k], :, where(j)]
        return remote(piece, piece, ag_s.at[k, 0], ag_r.at[k, j], me_r, j * stride)

    def fsend(k, j):
        piece = fac.at[k, bits[k], :, where(j)]
        return remote(piece, piece, fw_s.at[k, j], fw_r.at[k, j], partners[k], me_s)

    def fwait(k, j):
        piece = fac.at[k, 1 - bits[k], :, where(j)]
        return remote(piece, piece, fw_s.at[k, j], fw_r.at[k, j], partners[k], me_s)

    order = [(me_j + 1 + i) % nown for i in range(nown)]

    def send_gram(k, differ):
        gbuf[k, me_s] = pack(exact(differ, padded(differ), NT))
        for o in range(1, nsh):
            gsend(k, o).start()

    def finish_basis(k, differ):
        for o in range(1, nsh):
            gwait(k, o).wait_recv()
        return whiten(unpack(slots(gbuf.at[k])), differ)

    def project(k, basis_half, j):
        product = signs[k] * jnp.dot(
            basis_half, cur[:, where(j)], preferred_element_type=F32
        )
        pbuf[k, 0, :, where(j)] = product[:half_rank]
        pbuf[k, 1, :, where(j)] = product[half_rank:]
        psend(k, j).start()

    def pass_on(k, j):
        psend(k, j).wait_recv()
        psum[k, j] = pbuf[k, bits[k], :, where(j)] + pin[k, j]

    def pass_out(k, i):
        pass_on(k, order[i])
        if i < nown - 1:
            rsend(k, order[i]).start()
        else:
            owner(lambda: rsend(k, order[i]).start(), negate=True)

    def reduce_and_send(k):
        def mine():
            for o in range(1, nsh):
                rwait(k, o).wait_recv()
            total = psum[k, me_j]
            for o in range(1, nsh):
                total = total + rsbuf[k, (me_s + o) % nsh]
            fac[k, bits[k], :, where(me_j)] = total
            for o in range(nsh - 1, 0, -1):
                asend(k, o).start()

        owner(mine)

    def relay(k, i):
        j = (me_j + i) % nown
        if i:
            await_piece(k, j).wait_recv()
        else:
            owner(lambda: await_piece(k, j).wait_recv(), negate=True)
        fsend(k, j).start()

    lag = 2
    swap(0).wait_recv()
    differ = signs[0] * (sketches[0] - skin[0])
    send_gram(0, differ)
    give_starts.wait_recv()
    other = jnp.zeros((rank, rows), F32)
    for c in range(nown):
        part = pl.ds(c * width, width)
        other = other + lax.dot_general(
            w1in[:, part].astype(BF16), cur[:, part], NT, preferred_element_type=F32
        )
    cross[...] = other
    give_cross.start()
    basis = finish_basis(0, differ)
    base[...] = basis
    give_base.start()
    basis_half = basis.astype(BF16)
    give_cross.wait_recv()
    mbuf[0, me_s] = pack(
        signs[0] * exact(sketches[1] - crossin[...], padded(basis_half.astype(F32)), NT)
    )
    for o in range(nsh):
        if o:
            msend(0, o).start()
        msend(1, o).start()
    for i in range(nown):
        project(0, basis_half, order[i])
        if i >= lag:
            pass_out(0, i - lag)
    for i in range(max(nown - lag, 0), nown):
        pass_out(0, i)
    bt[0] = stack_left(basis, -0.5 * signs[0])
    swap(1).wait_recv()
    give_base.wait_recv()
    for o in range(nsh):
        if o:
            mwait(0, o).wait_recv()
        mwait(1, o).wait_recv()
    fix = -0.5 * signs[0]

    def moved(sketch, group, base_rows):
        return sketch + fix * exact(
            unpack(slots(mbuf.at[group])), padded(base_rows), (((1,), (0,)), ((), ()))
        )

    differ = signs[1] * (moved(sketches[1], 0, basis) - moved(skin[1], 1, basein[...]))
    send_gram(1, differ)
    reduce_and_send(0)
    basis = finish_basis(1, differ)
    basis_half = basis.astype(BF16)

    def update(i):
        j = (me_j + i) % nown
        fwait(0, j).wait_recv()
        piece = jnp.concatenate([fac[0, 0, :, where(j)], fac[0, 1, :, where(j)]], axis=0)
        change = jnp.dot(bt[0], stack_right(piece), preferred_element_type=F32)
        cur[:, where(j)] = (cur[:, where(j)].astype(F32) + change).astype(BF16)
        project(1, basis_half, j)

    seq = list(range(1, nown)) + [0]
    relay(0, 0)
    for n in range(1, nown):
        relay(0, n)
    bt_out[...] = stack_left(basis, -0.5 * signs[1])
    for n in range(nown):
        update(seq[n])
        if n >= lag:
            pass_out(1, n - lag)
    for i in range(max(nown - lag, 0), nown):
        pass_out(1, i)
    reduce_and_send(1)
    for n in range(nown):
        relay(1, n)
    for n in range(nown):
        fwait(1, (me_j + n) % nown).wait_recv()

    give_starts.wait_send()
    give_cross.wait_send()
    give_base.wait_send()
    for o in range(nsh):
        if o:
            msend(0, o).wait_send()
        msend(1, o).wait_send()
    for k in range(STEPS):
        swap(k).wait_send()
        for o in range(1, nsh):
            gsend(k, o).wait_send()
        for i in range(nown):
            psend(k, order[i]).wait_send()
            fsend(k, order[i]).wait_send()
            if i < nown - 1:
                rsend(k, order[i]).wait_send()

    def sent_all():
        for k in range(STEPS):
            for o in range(1, nsh):
                asend(k, o).wait_send()

    def sent_own():
        for k in range(STEPS):
            rsend(k, me_j).wait_send()

    owner(sent_all)
    owner(sent_own, negate=True)


def update_kernel(cur, bt, fac, cur_out, fac_out, fresh, st_sem, fo_sem):
    pieces, _, width = fresh.shape
    factors = pltpu.make_async_copy(fac, fac_out, fo_sem)
    factors.start()

    def store(c):
        return pltpu.make_async_copy(
            fresh.at[c], cur_out.at[:, pl.ds(c * width, width)], st_sem.at[c]
        )

    for c in range(pieces):
        part = pl.ds(c * width, width)
        piece = jnp.concatenate([fac[STEPS - 1, 0, :, part], fac[STEPS - 1, 1, :, part]], axis=0)
        change = jnp.dot(bt[...], stack_right(piece), preferred_element_type=F32)
        fresh[c] = (cur[:, part].astype(F32) + change).astype(BF16)
        store(c).start()
    factors.wait()
    for c in range(pieces):
        store(c).wait()


def shards(weights, warm_start):
    nrep, nsh = lax.axis_size("rep"), lax.axis_size("shard")
    _, rows, cols = weights.shape
    rank = warm_start.shape[2]
    half = rank // 2
    nown = math.gcd(cols // LANES, nsh)
    width = cols // nown
    dma = pltpu.SemaphoreType.DMA
    held = 2 * rows * cols + 4 * STEPS * rank * cols + 2 * rows * LANES + 13000 * 1024
    hbm = pl.BlockSpec(memory_space=pltpu.HBM)
    vmem = pl.BlockSpec(memory_space=pltpu.VMEM)
    current, factors, bt = pl.pallas_call(
        functools.partial(comm_kernel, nrep, nsh, nown),
        out_shape=(
            jax.ShapeDtypeStruct((rows, cols), BF16),
            jax.ShapeDtypeStruct((STEPS, 2, half, cols), F32),
            jax.ShapeDtypeStruct((rows, LANES), BF16),
        ),
        in_specs=[hbm, hbm],
        out_specs=(vmem, vmem, vmem),
        scratch_shapes=[
            pltpu.VMEM(warm_start.shape[1:], BF16),
            pltpu.VMEM((STEPS, rank, rows), F32),
            pltpu.VMEM((STEPS, rank, rows), F32),
            pltpu.VMEM((rank, cols), F32),
            pltpu.VMEM((rank, cols), F32),
            pltpu.VMEM((rank, rows), F32),
            pltpu.VMEM((rank, rows), F32),
            pltpu.VMEM((rank, rows), F32),
            pltpu.VMEM((rank, rows), F32),
            pltpu.VMEM((STEPS, nsh, half, LANES), F32),
            pltpu.VMEM((STEPS, nsh, half, LANES), F32),
            pltpu.VMEM((STEPS, 2, half, cols), F32),
            pltpu.VMEM((STEPS, nown, half, width), F32),
            pltpu.VMEM((STEPS, nown, half, width), F32),
            pltpu.VMEM((STEPS, nsh, half, width), F32),
            pltpu.VMEM((1, rows, LANES), BF16),
            dma((nown,)),
            dma,
            dma((STEPS,)),
            dma((STEPS,)),
            dma,
            dma,
            dma,
            dma,
            dma,
            dma,
            dma((STEPS, nsh)),
            dma((STEPS, nsh)),
            dma((STEPS, nsh)),
            dma((STEPS, nsh)),
            dma((STEPS, nown)),
            dma((STEPS, nown)),
            dma((STEPS, nown)),
            dma((STEPS, nsh)),
            dma((STEPS, nsh)),
            dma((STEPS, nown)),
            dma((STEPS, nown)),
            dma((STEPS, nown)),
        ],
        compiler_params=pltpu.CompilerParams(
            collective_id=0, has_side_effects=True, vmem_limit_bytes=VMEM - held
        ),
        name="rounds",
    )(weights[0], warm_start[0])
    corrected, factors = pl.pallas_call(
        update_kernel,
        out_shape=(
            jax.ShapeDtypeStruct((rows, cols), BF16),
            jax.ShapeDtypeStruct((STEPS, 2, half, cols), F32),
        ),
        in_specs=[vmem, vmem, vmem],
        out_specs=(hbm, hbm),
        scratch_shapes=[
            pltpu.VMEM((nown, rows, width), BF16),
            dma((nown,)),
            dma,
        ],
        compiler_params=pltpu.CompilerParams(vmem_limit_bytes=32 * 1024 * 1024),
        name="update",
    )(current, bt, factors)
    return (corrected[None], factors.reshape(1, STEPS, rank, cols))


def solution(mesh):
    placed = (P("rep", "shard", None), P("rep", None, None, None))
    return jax.shard_map(
        shards,
        mesh=mesh,
        in_specs=placed,
        out_specs=(P("rep", "shard", None), P("rep", None, None, None)),
        check_vma=False,
    )
```
